32 devices in a mesh: dp: 8 (over y, x, core), tensor: 4 (over z).
Axes of the slice: x: 2, y: 2, z: 4, core: 2. Of those that a mesh axis runs over, the one named last changes fastest.
Arguments:
- block_in: bfloat16 [16, 584, 1024], P('dp', 'tensor'), may hold values from -6 to 6
- norm_gain: bfloat16 [2, 2, 1024], P(None, None, 'dp'), may hold values from 0.5 to 1.5
- norm_bias: bfloat16 [2, 2, 1024], P(None, None, 'dp'), may hold values from -1.5 to 1.5
- w_qkv: bfloat16 [2, 1024, 3, 1024], P(None, 'dp', None, 'tensor')
- w_out: bfloat16 [2, 1024, 1024], P(None, ('tensor', 'dp')), may hold values from -2 to 2
- w_up: bfloat16 [2, 1024, 4096], P(None, 'dp', 'tensor'), may hold values from -0.1875 to 0.1875
- w_down: bfloat16 [2, 4096, 1024], P(None, ('tensor', 'dp')), may hold values from -0.09375 to 0.09375
- cotangent: bfloat16 [16, 584, 1024], P('dp', 'tensor'), may hold values from -6 to 6
- valid: int32 [16], P('dp'), may hold values 0 or 1
- lengths: int32 [16], P('dp'), may hold values from 504 to 577, as said below
Outputs:
- block_out: bfloat16 [16, 584, 1024], P('dp', 'tensor')
- in_grad: float32 [16, 584, 1024], P('dp', 'tensor')
- grad_gain: float32 [2, 2, 1024], P(None, None, 'dp')
- grad_bias: float32 [2, 2, 1024], P(None, None, 'dp')
- grad_qkv: float32 [2, 1024, 3, 1024], P(None, 'dp', None, 'tensor')
- grad_out: float32 [2, 1024, 1024], P(None, ('tensor', 'dp'))
- grad_up: float32 [2, 1024, 4096], P(None, 'dp', 'tensor')
- grad_down: float32 [2, 4096, 1024], P(None, ('tensor', 'dp'))
The draws below stay inside these ranges and needn't reach their ends.
Inputs may be any that keep to these rules, and one draw needn't show every extreme that they name: `valid`: 1 marks a slot that holds an image, 0 a padding slot. Positions from lengths[i] on are padding; some slot has exactly 577 tokens.
All inputs are finite; a program needn't handle non-finite values. No bound on the sum of `valid` on one device may be relied on, other than what follows from the above.
Results may differ from the reference program's by a relative error of at most 0.024.
Values may be sent and summed in bfloat16 or wider, within the bound.
No kernel may reach another device: no remote copies, remote signals or barrier semaphores. Data moves between devices by JAX's collectives and lax.ppermute only.
A program may use at most 192 MiB of HBM per device.

```python
import jax
import jax.numpy as jnp
from jax import lax

D = 1024
HEADS = 16
HEAD_DIM = 64
FF = 4096
SEQ = 584
TOKMAX = 577
LAYERS = 2
SLOTS = 16


def draw_w_qkv(key, part):
    base = jax.random.normal(key, (LAYERS, D, 3, D), jnp.float32) * D ** (-0.5)
    return base.astype(jnp.bfloat16)


def draw_lengths(key, part):
    lowest = TOKMAX - SEQ // 8
    drawn = jax.random.randint(key, (SLOTS,), lowest, TOKMAX + 1).astype(jnp.int32)
    drawn = drawn.at[0].set(TOKMAX)
    return drawn.at[1].set(lowest)


def touch_ends(values, rng, least, high):
    place = [jax.random.randint(jax.random.fold_in(rng, axis), (), 0, length) for axis, length in enumerate(values.shape)]
    widest = values.shape.index(max(values.shape))
    next_to = place[:widest] + [(place[widest] + 1) % values.shape[widest]] + place[widest + 1:]
    return values.at[tuple(place)].set(least).at[tuple(next_to)].set(high)


def shard_levels(own_key, extent, shards, low, high):
    factor_of, own = 1.0, jax.random.fold_in(own_key, 6)
    for axis_at, parts in shards:
        steps = jnp.exp(jax.random.uniform(jax.random.fold_in(own, axis_at), (parts,), jnp.float32, low / len(shards), high / len(shards)))
        factor_of = factor_of * jnp.repeat(steps, extent[axis_at] // parts).reshape([-1 if axis == axis_at else 1 for axis in range(len(extent))])
    return factor_of


def noise(key, dims, width, bound, split=(), held_as=jnp.bfloat16):
    values = jax.random.normal(key, dims, jnp.float32) * width
    if len(split) > 0:
        values = shard_levels(key, dims, split, -0.22, 0.18) * values
    return jnp.clip(values, min=-bound, max=bound).astype(held_as)


def setup_inputs(seed: int = 0) -> dict:
    key_list = jax.random.split(jax.random.key(seed), 11)
    return {
        "block_in": noise(key_list[0], (SLOTS, SEQ, D), 1.0, 6.0, ((0, 8), (1, 4))),
        "norm_gain": jnp.clip(1.0 + 0.1 * jax.random.normal(key_list[1], (LAYERS, 2, D), jnp.float32), 0.5, 1.5).astype(jnp.bfloat16),
        "norm_bias": noise(key_list[2], (LAYERS, 2, D), 0.3, 1.5, ((2, 8),)),
        "w_qkv": draw_w_qkv(jax.random.fold_in(key_list[10], 71), 0),
        "w_out": noise(key_list[4], (LAYERS, D, D), (max(1, D * 4 // SEQ)) ** -0.5, 2.0, ((1, 32),)),
        "w_up": noise(key_list[5], (LAYERS, D, FF), D ** -0.5, 0.1875, ((1, 8), (2, 4))),
        "w_down": noise(key_list[6], (LAYERS, FF, D), FF ** -0.5, 0.09375, ((1, 32),)),
        "cotangent": noise(key_list[7], (SLOTS, SEQ, D), 1.0, 6.0, ((0, 8), (1, 4))),
        "valid": touch_ends((jax.random.randint(key_list[8], (SLOTS,), 0, 8) < 7).astype(jnp.int32), jax.random.fold_in(key_list[8], 1), 0, 1),
        "lengths": draw_lengths(jax.random.fold_in(key_list[10], 71), 0),
    }


epsilon = 1e-06
root_half = 0.7071067811865476
density = 0.3989422804014327

def normalize(stream, gain_row, bias_row):
    center = stream - lax.optimization_barrier(jnp.mean(stream, axis=-1, keepdims=True))
    inverse = lax.rsqrt(lax.optimization_barrier(jnp.mean(center * center, axis=-1, keepdims=True)) + epsilon)
    scaled = center * inverse
    return (scaled * gain_row + bias_row, scaled, inverse)

def norm_back(upstream, scaled, inverse, gain_row):
    scaled_grad = upstream * gain_row
    mean_grad = lax.optimization_barrier(jnp.mean(scaled_grad, axis=-1, keepdims=True))
    second = lax.optimization_barrier(jnp.mean(scaled_grad * scaled, axis=-1, keepdims=True))
    leading = tuple(range(upstream.ndim - 1))
    return (inverse * (scaled_grad - mean_grad - scaled * second), lax.optimization_barrier(jnp.sum(upstream * scaled, axis=leading)), lax.optimization_barrier(jnp.sum(upstream, axis=leading)))

def gelu_pair(inputs):
    cumulative = 0.5 * (1.0 + lax.erf(inputs * root_half))
    return (inputs * cumulative, cumulative + inputs * jnp.exp(-0.5 * inputs * inputs) * density)

def image_scores(packed, key_mask):
    queries = packed[:, 0].astype(jnp.float32)
    key_rows = packed[:, 1].astype(jnp.float32)
    scores = jnp.einsum('qhe,khe->hqk', queries, key_rows) * HEAD_DIM ** (-0.5)
    return jnp.where(key_mask[None, None, :], scores, -1e+30)

def attend_image(packed, key_mask):
    scores = image_scores(packed, key_mask)
    largest = lax.optimization_barrier(jnp.max(scores, axis=-1, keepdims=True))
    denominator = lax.optimization_barrier(jnp.sum(jnp.exp(scores - largest), axis=-1, keepdims=True))
    log_total = largest + jnp.log(denominator)
    attn_probs = lax.optimization_barrier(jnp.exp(scores - log_total).astype(jnp.bfloat16)).astype(jnp.float32)
    context = jnp.einsum('hqk,khe->qhe', attn_probs, packed[:, 2].astype(jnp.float32))
    return (context.astype(jnp.bfloat16), log_total[:, :, 0])

def attend_back_image(packed, log_total, grad_context, key_mask):
    scores = image_scores(packed, key_mask)
    attn_probs = jnp.exp(scores - log_total[:, :, None])
    rounded = lax.optimization_barrier(attn_probs.astype(jnp.bfloat16)).astype(jnp.float32)
    grad_ctx32 = grad_context.astype(jnp.float32)
    grad_values = jnp.einsum('hqk,qhe->khe', rounded, grad_ctx32)
    grad_probs = jnp.einsum('qhe,khe->hqk', grad_ctx32, packed[:, 2].astype(jnp.float32))
    row_delta = lax.optimization_barrier(jnp.sum(attn_probs * grad_probs, axis=-1, keepdims=True))
    grad_scores = lax.optimization_barrier((attn_probs * (grad_probs - row_delta)).astype(jnp.bfloat16)).astype(jnp.float32)
    grad_queries = jnp.einsum('hqk,khe->qhe', grad_scores, packed[:, 1].astype(jnp.float32)) * HEAD_DIM ** (-0.5)
    grad_keys = jnp.einsum('hqk,qhe->khe', grad_scores, packed[:, 0].astype(jnp.float32)) * HEAD_DIM ** (-0.5)
    return jnp.stack([grad_queries, grad_keys, grad_values], axis=1).astype(jnp.bfloat16)

def reference(block_in, norm_gain, norm_bias, w_qkv, w_out, w_up, w_down, cotangent, valid, lengths):
    all_rows = SLOTS * SEQ
    positions = jnp.arange(SEQ, dtype=jnp.int32)
    key_masks = positions[None, :] < lengths[:, None]
    row_mask = jnp.where(key_masks & (valid[:, None] > 0), 1.0, 0.0).astype(jnp.float32)
    row_mask = row_mask.reshape(all_rows, 1)
    stream = block_in.astype(jnp.float32).reshape(all_rows, D)
    stored = []
    for layer_index in range(LAYERS):
        gain_rows = norm_gain[layer_index].astype(jnp.float32)
        bias_rows = norm_bias[layer_index].astype(jnp.float32)
        qkv_flat = w_qkv[layer_index].reshape(D, 3 * D)
        normed_one, scaled_one, inverse_one = normalize(stream, gain_rows[0], bias_rows[0])
        normed_one = normed_one.astype(jnp.bfloat16)
        packed = jnp.dot(normed_one, qkv_flat, preferred_element_type=jnp.float32).astype(jnp.bfloat16)
        packed = packed.reshape(SLOTS, SEQ, 3, HEADS, HEAD_DIM)
        context, log_totals = lax.map(lambda member: attend_image(member[0], member[1]), (packed, key_masks))
        context_flat = context.reshape(all_rows, D)
        middle = stream + jnp.dot(context_flat, w_out[layer_index], preferred_element_type=jnp.float32)
        normed_two, scaled_two, inverse_two = normalize(middle, gain_rows[1], bias_rows[1])
        normed_two = normed_two.astype(jnp.bfloat16)
        activated, gelu_slope = gelu_pair(jnp.dot(normed_two, w_up[layer_index], preferred_element_type=jnp.float32))
        hidden = activated.astype(jnp.bfloat16)
        stored.append((scaled_one, inverse_one, normed_one, packed, log_totals, context_flat, scaled_two, inverse_two, normed_two, gelu_slope, hidden))
        stream = middle + jnp.dot(hidden, w_down[layer_index], preferred_element_type=jnp.float32)
    block_out = (stream * row_mask).astype(jnp.bfloat16).reshape(SLOTS, SEQ, D)
    gradient = cotangent.astype(jnp.float32).reshape(all_rows, D) * row_mask
    results = [None] * LAYERS
    for layer_index in reversed(range(LAYERS)):
        scaled_one, inverse_one, normed_one, packed, log_totals, context_flat, scaled_two, inverse_two, normed_two, gelu_slope, hidden = stored[layer_index]
        gain_rows = norm_gain[layer_index].astype(jnp.float32)
        qkv_flat = w_qkv[layer_index].reshape(D, 3 * D)
        dy_two = gradient.astype(jnp.bfloat16)
        grad_down = jnp.dot(hidden.T, dy_two, preferred_element_type=jnp.float32)
        grad_up_in = (jnp.dot(dy_two, w_down[layer_index].T, preferred_element_type=jnp.float32) * gelu_slope).astype(jnp.bfloat16)
        grad_up = jnp.dot(normed_two.T, grad_up_in, preferred_element_type=jnp.float32)
        grad_normed_two = jnp.dot(grad_up_in, w_up[layer_index].T, preferred_element_type=jnp.float32)
        back_two, gain_two, bias_two = norm_back(grad_normed_two, scaled_two, inverse_two, gain_rows[1])
        gradient = gradient + back_two
        dy_one = gradient.astype(jnp.bfloat16)
        grad_out = jnp.dot(context_flat.T, dy_one, preferred_element_type=jnp.float32)
        grad_context = jnp.dot(dy_one, w_out[layer_index].T, preferred_element_type=jnp.float32).astype(jnp.bfloat16)
        grad_context = grad_context.reshape(SLOTS, SEQ, HEADS, HEAD_DIM)
        grad_packed = lax.map(lambda member: attend_back_image(member[0], member[1], member[2], member[3]), (packed, log_totals, grad_context, key_masks))
        grad_packed = grad_packed.reshape(all_rows, 3 * D)
        grad_qkv = jnp.dot(normed_one.T, grad_packed, preferred_element_type=jnp.float32).reshape(D, 3, D)
        grad_normed_one = jnp.dot(grad_packed, qkv_flat.T, preferred_element_type=jnp.float32)
        back_one, gain_one, bias_one = norm_back(grad_normed_one, scaled_one, inverse_one, gain_rows[0])
        gradient = gradient + back_one
        results[layer_index] = (jnp.stack([gain_one, gain_two]), jnp.stack([bias_one, bias_two]), grad_qkv, grad_out, grad_up, grad_down)
    in_grad = gradient.reshape(SLOTS, SEQ, D)
    return (block_out, in_grad, jnp.stack([entry[0] for entry in results]), jnp.stack([entry[1] for entry in results]), jnp.stack([entry[2] for entry in results]), jnp.stack([entry[3] for entry in results]), jnp.stack([entry[4] for entry in results]), jnp.stack([entry[5] for entry in results]))
```

```python
import functools

import jax
import jax.numpy as jnp
from jax import lax
from jax.experimental import pallas as pl
from jax.experimental.pallas import tpu as pltpu
from jax.sharding import PartitionSpec as P

HEAD_DIM = 64
PAD_TO = 8

epsilon = 1e-06
root_half = 0.7071067811865476
density = 0.3989422804014327
f32 = jnp.float32
bf16 = jnp.bfloat16


def normalize(stream, gain_row, bias_row):
    center = stream - jnp.mean(stream, axis=-1, keepdims=True)
    inverse = lax.rsqrt(jnp.mean(center * center, axis=-1, keepdims=True) + epsilon)
    scaled = center * inverse
    return (scaled * gain_row + bias_row, scaled, inverse)


def norm_back(upstream, scaled, inverse, gain_row):
    scaled_grad = upstream * gain_row
    mean_grad = jnp.mean(scaled_grad, axis=-1, keepdims=True)
    second = jnp.mean(scaled_grad * scaled, axis=-1, keepdims=True)
    return (
        inverse * (scaled_grad - mean_grad - scaled * second),
        jnp.sum(upstream * scaled, axis=0),
        jnp.sum(upstream, axis=0),
    )


def gelu_pair(inputs):
    cumulative = 0.5 * (1.0 + lax.erf(inputs * root_half))
    return (inputs * cumulative, cumulative + inputs * jnp.exp(-0.5 * inputs * inputs) * density)


def dot_tt(a, b):
    return lax.dot_general(a, b, (((1,), (1,)), ((), ())), preferred_element_type=f32)


def dot_nn(a, b):
    return lax.dot_general(a, b, (((1,), (0,)), ((), ())), preferred_element_type=f32)


def dot_kk(a, b):
    return lax.dot_general(a, b, (((0,), (0,)), ((), ())), preferred_element_type=f32)


def head_probs(q, k, mask_row):
    scores = dot_tt(q, k) * (HEAD_DIM ** (-0.5))
    scores = jnp.where(mask_row > 0.0, scores, -1e30)
    largest = jnp.max(scores, axis=-1, keepdims=True)
    numer = jnp.exp(scores - largest)
    return numer * (1.0 / jnp.sum(numer, axis=-1, keepdims=True))


def attend_kernel(q_ref, k_ref, v_ref, mask_ref, out_ref):
    mask_row = mask_ref[0:1, :]
    for at in range(0, q_ref.shape[1], HEAD_DIM):
        cols = slice(at, at + HEAD_DIM)
        probs = head_probs(q_ref[:, cols], k_ref[:, cols], mask_row).astype(bf16)
        out_ref[:, cols] = dot_nn(probs, v_ref[:, cols]).astype(bf16)


def attend(packed, mask):
    rows, wide = packed.shape
    width = wide // 3
    block = 2 * HEAD_DIM
    steps = width // block
    return pl.pallas_call(
        attend_kernel,
        out_shape=jax.ShapeDtypeStruct((rows, width), bf16),
        grid=(steps,),
        in_specs=[
            pl.BlockSpec((rows, block), lambda h: (0, h)),
            pl.BlockSpec((rows, block), lambda h: (0, h + steps)),
            pl.BlockSpec((rows, block), lambda h: (0, h + 2 * steps)),
            pl.BlockSpec(mask.shape, lambda h: (0, 0)),
        ],
        out_specs=pl.BlockSpec((rows, block), lambda h: (0, h)),
        cost_estimate=pl.CostEstimate(
            flops=4 * rows * rows * width,
            bytes_accessed=8 * rows * width,
            transcendentals=rows * rows * (width // HEAD_DIM),
        ),
        name="attend",
    )(packed, packed, packed, mask)


def attend_back_kernel(q_ref, k_ref, v_ref, g_ref, mask_ref, out_ref):
    mask_row = mask_ref[0:1, :]
    step = pl.program_id(0)
    block = q_ref.shape[1]
    width = out_ref.shape[1] // 3
    scale = HEAD_DIM ** (-0.5)
    grads = ([], [], [])
    for at in range(0, block, HEAD_DIM):
        cols = slice(at, at + HEAD_DIM)
        q, k, v, g = (ref[:, cols] for ref in (q_ref, k_ref, v_ref, g_ref))
        probs = head_probs(q, k, mask_row)
        grads[2].append(dot_kk(probs.astype(bf16), g))
        grad_probs = dot_tt(g, v)
        row_delta = jnp.sum(probs * grad_probs, axis=-1, keepdims=True)
        grad_scores = (probs * (grad_probs - row_delta)).astype(bf16)
        grads[0].append(dot_nn(grad_scores, k) * scale)
        grads[1].append(dot_kk(grad_scores, q) * scale)
    for part in range(3):
        start = pl.multiple_of(part * width + step * block, block)
        out_ref[:, pl.ds(start, block)] = jnp.concatenate(grads[part], axis=1).astype(bf16)


def attend_back(packed, grad_context, mask):
    rows, wide = packed.shape
    width = wide // 3
    block = 2 * HEAD_DIM
    steps = width // block
    return pl.pallas_call(
        attend_back_kernel,
        out_shape=jax.ShapeDtypeStruct((rows, wide), bf16),
        grid=(steps,),
        in_specs=[
            pl.BlockSpec((rows, block), lambda h: (0, h)),
            pl.BlockSpec((rows, block), lambda h: (0, h + steps)),
            pl.BlockSpec((rows, block), lambda h: (0, h + 2 * steps)),
            pl.BlockSpec((rows, block), lambda h: (0, h)),
            pl.BlockSpec(mask.shape, lambda h: (0, 0)),
        ],
        out_specs=pl.BlockSpec((rows, wide), lambda h: (0, 0)),
        cost_estimate=pl.CostEstimate(
            flops=10 * rows * rows * width,
            bytes_accessed=14 * rows * width,
            transcendentals=rows * rows * (width // HEAD_DIM),
        ),
        name="attend_back",
    )(packed, packed, packed, grad_context, mask)


def shift(value, axis, by):
    size = lax.axis_size(axis)
    return lax.ppermute(value, axis, [(i, (i + by) % size) for i in range(size)])


def along_x(value, axis):
    size = lax.axis_size("x")
    if size <= 2:
        return value
    order = (lax.axis_index("x") - jnp.arange(size, dtype=jnp.int32)) % size
    return jnp.take(value, order, axis=axis)


def gather_rows(own, path):
    nx, nz = lax.axis_size("x"), lax.axis_size("z")
    column = jnp.stack([own] + [shift(own, "z", r) for r in range(1, nz)])
    here = [column] + [shift(column, "x", j) for j in range(1, nx)]
    there = [shift(column, "y", 1)]
    for j in range(1, nx):
        there.append(shift(here[j], "y", 1) if path == 0 else shift(there[0], "x", j))
    return [here, there]


def scatter_rows(slots, path):
    nx, nz = lax.axis_size("x"), lax.axis_size("z")
    here, there = list(slots[0]), list(slots[1])
    add = lambda a, b: (a.astype(f32) + b.astype(f32)).astype(bf16)
    for j in range(1, nx):
        if path == 0:
            here[j] = add(here[j], shift(there[j], "y", 1))
        else:
            there[0] = add(there[0], shift(there[j], "x", -j))
    column = here[0].astype(f32) + shift(there[0], "y", 1).astype(f32)
    for j in range(1, nx):
        column = column + shift(here[j], "x", -j).astype(f32)
    column = column.astype(bf16)
    total = column[0].astype(f32)
    for r in range(1, nz):
        total = total + shift(column[r], "z", -r).astype(f32)
    return total


def sum_all(value):
    for axis in ("core", "y", "x", "z"):
        total = value
        for by in range(1, lax.axis_size(axis)):
            total = total + shift(value, axis, by)
        value = total
    return value


def widen(own):
    return jnp.concatenate([own, shift(own, "core", 1)], axis=0)


def narrow(partial_sum):
    rows = partial_sum.shape[0] // 2
    other = shift(partial_sum[rows:].astype(bf16), "core", 1)
    return partial_sum[:rows] + other.astype(f32)


def image_pairs(message, images, nz):
    pairs = []
    for core in range(2):
        for place in range(nz):
            image = (place + message) % images
            pairs.append((core * nz + place, (place // images) * nz + images * core + image))
    return pairs


def to_images(local):
    images, short, width = local.shape
    place = lax.axis_index("z")
    nz = lax.axis_size("z")
    received = []
    for message in range(images):
        sent = lax.dynamic_index_in_dim(local, (place + message) % images, 0, keepdims=False)
        received.append(lax.ppermute(sent, ("core", "z"), image_pairs(message, images, nz)))
    parts = []
    for quarter in range(images):
        part = received[0]
        for message in range(1, images):
            part = jnp.where((place - message) % images == quarter, received[message], part)
        parts.append(part)
    rows = images * short
    padded = -(-rows // PAD_TO) * PAD_TO
    if padded > rows:
        parts.append(jnp.zeros((padded - rows, width), local.dtype))
    return jnp.concatenate(parts, axis=0)


def from_images(own, images, short):
    place = lax.axis_index("z")
    nz = lax.axis_size("z")
    quarters = [own[q * short : (q + 1) * short] for q in range(images)]
    received = []
    for message in range(images):
        sent = quarters[0]
        for quarter in range(1, images):
            sent = jnp.where((place - message) % images == quarter, quarters[quarter], sent)
        back = [(b, a) for a, b in image_pairs(message, images, nz)]
        received.append(lax.ppermute(sent, ("core", "z"), back))
    outs = []
    for image in range(images):
        out = received[0]
        for message in range(1, images):
            out = jnp.where((place + message) % images == image, received[message], out)
        outs.append(out)
    return jnp.stack(outs)


def own_index():
    return (lax.axis_index("y") * lax.axis_size("x") + lax.axis_index("x")) * 2 + lax.axis_index(
        "core"
    )


def to_rows(w_qkv, w_up):
    layers, depth, _, qkv_cols = w_qkv.shape
    nx = lax.axis_size("x")
    dp = 4 * nx
    head_rows = qkv_cols // dp
    up_rows = w_up.shape[2] // dp
    qkv = w_qkv.reshape(layers, depth, 3, 2, nx, 2, head_rows)
    qkv = qkv.transpose(5, 4, 3, 0, 2, 6, 1).reshape(dp, layers, 3 * head_rows, depth)
    up = w_up.reshape(layers, depth, dp, up_rows).transpose(2, 0, 3, 1)
    sent = jnp.concatenate([qkv, up], axis=2)
    got = lax.all_to_all(sent, ("y", "x", "core"), 0, 0, tiled=True)
    got = got.transpose(1, 2, 0, 3).reshape(layers, 3 * head_rows + up_rows, dp * depth)
    return got[:, : 3 * head_rows], got[:, 3 * head_rows :]


def from_rows(own_qkv, own_up, qkv_cols, up_cols):
    nx = lax.axis_size("x")
    dp = 4 * nx
    width = own_qkv.shape[1]
    depth = width // dp
    head_rows = qkv_cols // dp
    up_rows = up_cols // dp
    sent = jnp.concatenate([own_qkv, own_up], axis=0).astype(bf16)
    sent = sent.reshape(-1, dp, depth).transpose(1, 0, 2)
    got = lax.all_to_all(sent, ("y", "x", "core"), 0, 0, tiled=True).astype(f32)
    qkv = got[:, : 3 * head_rows].reshape(2, nx, 2, 3, head_rows, depth)
    qkv = qkv.transpose(5, 3, 2, 1, 0, 4).reshape(depth, 3, qkv_cols)
    up = got[:, 3 * head_rows :].transpose(2, 0, 1).reshape(depth, up_cols)
    return qkv, up


def swap_pairs():
    return [(y * 2 + c, c * 2 + y) for y in range(2) for c in range(2)]


def join_heads(slots, parts):
    nx, nz = lax.axis_size("x"), lax.axis_size("z")
    stack = jnp.stack([jnp.stack(line) for line in slots])
    rows = stack.shape[3] // parts
    width = stack.shape[4]
    stack = along_x(stack, 1).reshape(2, nx, nz, parts, rows, width)
    return stack.transpose(3, 2, 1, 0, 4, 5).reshape(parts * nz * nx * 2 * rows, width)


def split_heads(joined, parts):
    nx, nz = lax.axis_size("x"), lax.axis_size("z")
    width = joined.shape[1]
    rows = joined.shape[0] // (parts * nz * nx * 2)
    stack = joined.reshape(parts, nz, nx, 2, rows, width).transpose(3, 2, 1, 0, 4, 5)
    stack = along_x(stack.reshape(2, nx, nz, parts * rows, width), 1)
    return [[stack[i, j] for j in range(nx)] for i in range(2)]


def join_units(slots):
    width = slots[0][0].shape[-1]
    return jnp.concatenate([s.reshape(-1, width) for line in slots for s in line], axis=0)


def split_units(joined):
    nx, nz = lax.axis_size("x"), lax.axis_size("z")
    stack = joined.reshape(2, nx, nz, -1, joined.shape[1])
    return [[stack[i, j] for j in range(nx)] for i in range(2)]


def body(block_in, norm_gain, norm_bias, w_qkv, w_out, w_up, w_down, cotangent, valid, lengths):
    images, short, model_width = block_in.shape
    layers = w_qkv.shape[0]
    qkv_cols, up_cols = w_qkv.shape[3], w_up.shape[2]
    core, place = lax.axis_index("core"), lax.axis_index("z")

    both = jnp.stack([lengths, valid])
    other = shift(both, "core", 1)
    pair = jnp.where(core == 0, jnp.concatenate([both, other], 1), jnp.concatenate([other, both], 1))
    mine = lax.dynamic_index_in_dim(pair, place, 1, keepdims=False)
    length, is_valid = mine[0], mine[1]

    rows = images * short
    padded = -(-rows // PAD_TO) * PAD_TO
    within = jnp.arange(padded, dtype=jnp.int32)
    place_of = lambda which: jnp.where(within < rows, which * rows + within, 2 * rows)
    key_places = jnp.concatenate([place_of(core), place_of(1 - core)])
    mask = jnp.broadcast_to((key_places < length).astype(f32)[None, :], (8, 2 * padded))
    row_mask = ((place_of(core) < length) & (is_valid > 0)).astype(f32)[:, None]

    norms = lax.all_gather(
        jnp.stack([norm_gain, norm_bias]), ("y", "x", "core"), axis=3, tiled=True
    ).astype(f32)
    gains, biases = norms[0], norms[1]

    stream = to_images(block_in).astype(f32)
    rows_qkv, rows_up = to_rows(w_qkv, w_up)
    rows_out = lax.ppermute(w_out, ("y", "core"), swap_pairs())

    weights = []
    for layer in range(layers):
        qkv = join_heads(gather_rows(rows_qkv[layer], layer % 2), 3)
        out = join_heads(gather_rows(rows_out[layer], 1 - layer % 2), 1)
        up = join_units(gather_rows(rows_up[layer], 0))
        down = join_units(gather_rows(w_down[layer], 1))
        weights.append((qkv, out, up, down))
    gradient_in = to_images(cotangent)

    stored = []
    for layer in range(layers):
        qkv, out, up, down = weights[layer]
        normed_one, scaled_one, inverse_one = normalize(
            stream, gains[layer, 0], biases[layer, 0]
        )
        wide_one = widen(normed_one.astype(bf16))
        packed = dot_tt(wide_one, qkv).astype(bf16)
        context = attend(packed, mask)
        middle = stream + narrow(dot_nn(context, out))
        normed_two, scaled_two, inverse_two = normalize(
            middle, gains[layer, 1], biases[layer, 1]
        )
        wide_two = widen(normed_two.astype(bf16))
        activated, slope = gelu_pair(dot_tt(wide_two, up))
        hidden = activated.astype(bf16)
        stored.append(
            (scaled_one, inverse_one, wide_one, packed, context,
             scaled_two, inverse_two, wide_two, slope, hidden)
        )
        stream = middle + narrow(dot_nn(hidden, down))
    block_out = from_images((stream * row_mask).astype(bf16), images, short)

    gradient = gradient_in.astype(f32) * row_mask
    norm_sums = [None] * layers
    owned = [None] * layers
    for layer in reversed(range(layers)):
        qkv, out, up, down = weights[layer]
        (scaled_one, inverse_one, wide_one, packed, context,
         scaled_two, inverse_two, wide_two, slope, hidden) = stored[layer]
        dy_two = widen(gradient.astype(bf16))
        grad_down = split_units(dot_kk(hidden, dy_two).astype(bf16))
        own_down = scatter_rows(grad_down, 1)
        grad_up_in = (dot_tt(dy_two, down) * slope).astype(bf16)
        grad_up = split_units(dot_kk(grad_up_in, wide_two).astype(bf16))
        own_up = scatter_rows(grad_up, 0)
        back_two, gain_two, bias_two = norm_back(
            narrow(dot_nn(grad_up_in, up)), scaled_two, inverse_two, gains[layer, 1]
        )
        gradient = gradient + back_two
        dy_one = widen(gradient.astype(bf16))
        grad_out = split_heads(dot_kk(context, dy_one).astype(bf16), 1)
        own_out = scatter_rows(grad_out, 1 - layer % 2)
        grad_context = dot_tt(dy_one, out).astype(bf16)
        grad_packed = attend_back(packed, grad_context, mask)
        grad_qkv = split_heads(dot_kk(grad_packed, wide_one).astype(bf16), 3)
        own_qkv = scatter_rows(grad_qkv, layer % 2)
        back_one, gain_one, bias_one = norm_back(
            narrow(dot_nn(grad_packed, qkv)), scaled_one, inverse_one, gains[layer, 0]
        )
        gradient = gradient + back_one
        norm_sums[layer] = jnp.stack([gain_one, gain_two, bias_one, bias_two])
        local_qkv, local_up = from_rows(own_qkv, own_up, qkv_cols, up_cols)
        local_out = lax.ppermute(own_out.astype(bf16), ("y", "core"), swap_pairs()).astype(f32)
        owned[layer] = (local_qkv, local_out, local_up, own_down)

    in_grad = from_images(gradient.astype(bf16), images, short).astype(f32)
    sums = sum_all(jnp.stack(norm_sums))
    depth = norm_gain.shape[2]
    sums = lax.dynamic_slice_in_dim(sums, own_index() * depth, depth, axis=2)
    return (
        block_out,
        in_grad,
        sums[:, :2],
        sums[:, 2:],
        jnp.stack([entry[0] for entry in owned]),
        jnp.stack([entry[1] for entry in owned]),
        jnp.stack([entry[2] for entry in owned]),
        jnp.stack([entry[3] for entry in owned]),
    )


def solution(mesh):
    dp, tensor = mesh.shape["dp"], mesh.shape["tensor"]
    split = jax.sharding.Mesh(
        mesh.devices.reshape(2, dp // 4, 2, tensor), ("y", "x", "core", "z")
    )
    d, t = ("y", "x", "core"), "z"
    in_specs = (
        P(d, t, None),
        P(None, None, d),
        P(None, None, d),
        P(None, d, None, t),
        P(None, (t,) + d, None),
        P(None, d, t),
        P(None, (t,) + d, None),
        P(d, t, None),
        P(d),
        P(d),
    )
    out_specs = (
        P(d, t, None),
        P(d, t, None),
        P(None, None, d),
        P(None, None, d),
        P(None, d, None, t),
        P(None, (t,) + d, None),
        P(None, d, t),
        P(None, (t,) + d, None),
    )
    return jax.shard_map(body, mesh=split, in_specs=in_specs, out_specs=out_specs, check_vma=False)
```
